128 devices in a mesh: grp: 8 (over x, core), exp: 16 (over y, z).
Axes of the slice: x: 4, y: 4, z: 4, core: 2. Of those that a mesh axis runs over, the one named last changes fastest.
Arguments:
- tokens: bfloat16 [16384, 2048], P(('grp', 'exp')), may hold values from -6 to 6
- grad_out: bfloat16 [16384, 2048], P(('grp', 'exp')), may hold values from -6 to 6
- probs: bfloat16 [16384, 6], P(('grp', 'exp')), may hold values from 0.049804688 to 0.3984375
- expert_ids: int32 [16384, 6], P(('grp', 'exp')), may hold values from 0 to 31, as said below
- serve_map: int32 [8, 16], replicated, may hold values from 0 to 1, as said below
- replica_pick: int32 [16384, 6], P(('grp', 'exp')), may hold values from 0 to 839
- w_gate: bfloat16 [32, 2048, 768], P('exp'), may hold values from -0.125 to 0.125
- w_up: bfloat16 [32, 2048, 768], P('exp'), may hold values from -0.125 to 0.125
- w_down: bfloat16 [32, 2048, 768], P('exp'), may hold values from -0.21875 to 0.21875
Outputs:
- grad_tokens: bfloat16 [16384, 2048], P(('grp', 'exp'))
- grad_probs: bfloat16 [16384, 6], P(('grp', 'exp'))
- grad_gate: float32 [32, 2048, 768], P('exp', 'grp')
- grad_up: float32 [32, 2048, 768], P('exp', 'grp')
- grad_down: float32 [32, 2048, 768], P('exp', 'grp')
The draws below stay inside these ranges and needn't reach their ends.
Inputs may be any that keep to these rules, and one draw needn't show every extreme that they name: `serve_map`: entry (g, c) names which of the experts c * 2 + entry the device of group g and column c serves; every expert is served by at least one group. `expert_ids`: each token names 6 different experts.
All inputs are finite; a program needn't handle non-finite values.
Results may differ from the reference program's by a relative error of at most 0.014.
Values may be sent and summed in bfloat16 or wider, within the bound.
A program may use at most 128 MiB of HBM per device.

```python
import jax
import jax.numpy as jnp
from jax import lax

D = 2048
FF_WIN = 768
EXP_DEV = 2
TOPK = 6
TOK_DEV = 128
EXPERTS = 32
TOKENS = 16384
CAP = 8
N_GRP = 8
N_EXP = 16


def column_plan(key):
    base_key = jax.random.fold_in(key, 11)
    first_key, perm_key, noise_key = jax.random.split(base_key, 3)
    first_count = jax.random.randint(first_key, (N_EXP,), 1, N_GRP)
    perm_keys = jax.random.split(perm_key, N_EXP)
    position = jax.vmap(lambda sub_key: jax.random.permutation(sub_key, N_GRP))(perm_keys)
    serve = (position.T >= first_count[None, :]).astype(jnp.int32)
    noise_factor = jax.random.randint(noise_key, (N_EXP * EXP_DEV,), 1, 4)
    return (serve, noise_factor)


def draw_serve_map(key, part):
    serve, noise_factor = column_plan(key)
    return serve


def draw_expert_ids(key, part):
    serve, noise_factor = column_plan(key)
    members = jnp.arange(EXPERTS, dtype=jnp.int32) % EXP_DEV
    columns = jnp.arange(EXPERTS, dtype=jnp.int32) // EXP_DEV
    replica_count = jnp.sum((serve[:, columns] == members[None, :]).astype(jnp.int32), axis=0)
    weight = replica_count * noise_factor
    raw_scores = jax.random.randint(jax.random.fold_in(key, 23), (TOKENS, EXPERTS), 1, 1048576)
    scores = raw_scores * weight[None, :] * EXPERTS + jnp.arange(EXPERTS, dtype=jnp.int32)[None, :]
    return lax.top_k(scores, TOPK)[1].astype(jnp.int32)


def plant(values, rng, least, top_value):
    longest = values.shape.index(max(values.shape))
    spots = []
    for shift in (0, 1):
        where = [jax.random.randint(jax.random.fold_in(rng, axis), (), 0, length) for axis, length in enumerate(values.shape)]
        where[longest] = (where[longest] + shift) % values.shape[longest]
        spots.append(tuple(where))
    return values.at[spots[0]].set(least).at[spots[1]].set(top_value)


def block_levels(own_key, shape, pieces, low, largest):
    def one(dim, blocks):
        steps = jax.random.uniform(jax.random.fold_in(jax.random.fold_in(own_key, 6), dim), (blocks,), jnp.float32, low / len(pieces), largest / len(pieces))
        return jnp.repeat(jnp.exp(steps), shape[dim] // blocks).reshape((-1,) + (1,) * (len(shape) - dim - 1))

    loudness = one(*pieces[0])
    for cut in pieces[1:]:
        loudness = loudness * one(*cut)
    return loudness


def noise(key, dims, width, reach, shards=(), kind=jnp.bfloat16):
    entries = jax.random.normal(key, dims, jnp.float32) * width
    if len(shards) > 0:
        entries = block_levels(key, dims, shards, -0.22, 0.18) * entries
    return jnp.clip(entries, min=-reach, max=reach).astype(kind)


def setup_inputs(seed: int = 0) -> dict:
    splits = jax.random.split(jax.random.key(seed), 10)
    tokens = noise(splits[0], (TOKENS, D), 1.0, 6.0, ((0, 128),))
    grad_out = noise(splits[1], (TOKENS, D), 1.0, 6.0, ((0, 128),))
    probs = jnp.clip(0.049804688 + 0.3486328 * jax.random.uniform(splits[2], (TOKENS, TOPK), jnp.float32) ** block_levels(splits[2], (TOKENS, TOPK), ((0, 128),), -0.2, 0.2), 0.049804688, 0.3984375).astype(jnp.bfloat16)
    expert_ids = draw_expert_ids(jax.random.fold_in(splits[9], 71), 0)
    serve_map = draw_serve_map(jax.random.fold_in(splits[9], 71), 0)
    replica_pick = plant(jax.random.randint(splits[5], (TOKENS, TOPK), 0, 840), jax.random.fold_in(splits[5], 1), 0, 839).astype(jnp.int32)
    w_gate = noise(splits[6], (EXPERTS, D, FF_WIN), D ** -0.5, 0.125, ((0, 16),))
    w_up = noise(splits[7], (EXPERTS, D, FF_WIN), D ** -0.5, 0.125, ((0, 16),))
    w_down = noise(splits[8], (EXPERTS, D, FF_WIN), FF_WIN ** -0.5, 0.21875, ((0, 16),))
    return dict(tokens=tokens, grad_out=grad_out, probs=probs, expert_ids=expert_ids, serve_map=serve_map, replica_pick=replica_pick, w_gate=w_gate, w_up=w_up, w_down=w_down)


def route_targets(expert_ids, serve_map, replica_pick):
    groups = serve_map.shape[0]
    columns = serve_map.shape[1]
    column = expert_ids // EXP_DEV
    member = expert_ids % EXP_DEV
    serving = (serve_map[:, column] == member[None]).astype(jnp.int32)
    order_index = (jnp.cumsum(serving, axis=0) - 1).astype(jnp.int32)
    server_count = jnp.sum(serving, axis=0).astype(jnp.int32)
    wanted = (replica_pick % server_count).astype(jnp.int32)
    chosen_group = serving * (order_index == wanted[None]).astype(jnp.int32)
    group_index = jnp.sum(chosen_group * jnp.arange(groups, dtype=jnp.int32)[:, None, None], axis=0)
    return (group_index * columns + column).astype(jnp.int32)


def route_ranks(target_flat, devices):
    onehot = (target_flat[:, None] == jnp.arange(devices, dtype=jnp.int32)[None, :]).astype(jnp.int32)
    running = jnp.cumsum(onehot, axis=0) - onehot
    return jnp.sum(running * onehot, axis=1).astype(jnp.int32)


def expert_backward(input_rows, grad_rows, prob_rows, weight_gate, weight_up, weight_down):
    contract = (((1,), (1,)), ((), ()))
    over_rows = (((0,), (0,)), ((), ()))
    gate = jnp.dot(input_rows, weight_gate, preferred_element_type=jnp.float32)
    up_value = jnp.dot(input_rows, weight_up, preferred_element_type=jnp.float32)
    sigmoid_gate = jax.nn.sigmoid(gate)
    silu_gate = gate * sigmoid_gate
    hidden = (silu_gate * up_value).astype(jnp.bfloat16)
    output = lax.dot_general(hidden, weight_down, contract, preferred_element_type=jnp.float32)
    route_prob = jnp.sum(grad_rows.astype(jnp.float32) * output, axis=1).astype(jnp.bfloat16)
    scaled = (prob_rows.astype(jnp.float32)[:, None] * grad_rows.astype(jnp.float32)).astype(jnp.bfloat16)
    grad_hidden = jnp.dot(scaled, weight_down, preferred_element_type=jnp.float32)
    grad_gate_pre = (grad_hidden * up_value * sigmoid_gate * (1.0 + gate * (1.0 - sigmoid_gate))).astype(jnp.bfloat16)
    grad_up_pre = (grad_hidden * silu_gate).astype(jnp.bfloat16)
    route_grad = lax.dot_general(grad_gate_pre, weight_gate, contract, preferred_element_type=jnp.float32)
    route_grad = (route_grad + lax.dot_general(grad_up_pre, weight_up, contract, preferred_element_type=jnp.float32)).astype(jnp.bfloat16)
    part_gate = lax.dot_general(input_rows, grad_gate_pre, over_rows, preferred_element_type=jnp.float32).astype(jnp.bfloat16)
    part_up = lax.dot_general(input_rows, grad_up_pre, over_rows, preferred_element_type=jnp.float32).astype(jnp.bfloat16)
    part_down = lax.dot_general(scaled, hidden, over_rows, preferred_element_type=jnp.float32).astype(jnp.bfloat16)
    return route_grad, route_prob, part_gate, part_up, part_down


def reference(tokens, grad_out, probs, expert_ids, serve_map, replica_pick, w_gate, w_up, w_down):
    groups = serve_map.shape[0]
    columns = serve_map.shape[1]
    devices = groups * columns
    buffer_rows = devices * CAP
    target = route_targets(expert_ids, serve_map, replica_pick)
    blocks = target.reshape(devices, TOK_DEV * TOPK)
    slot_rank = jax.vmap(lambda block_targets: route_ranks(block_targets, devices))(blocks).reshape(TOKENS, TOPK)
    kept_mask = slot_rank < CAP
    route_id = jnp.arange(TOKENS * TOPK, dtype=jnp.int32).reshape(TOKENS, TOPK)
    source = route_id // (TOK_DEV * TOPK)
    send_slot = (target * buffer_rows + source * CAP + slot_rank).astype(jnp.int32)
    send_slot = jnp.where(kept_mask, send_slot, devices * buffer_rows).astype(jnp.int32)
    slot_table = jnp.full((devices * buffer_rows,), -1, jnp.int32)
    slot_table = slot_table.at[send_slot.reshape(-1)].set(route_id.reshape(-1), mode="drop")
    slot_table = slot_table.reshape(devices, buffer_rows)
    flat_probs = probs.reshape(-1)

    def one_device(running_sums, scan_entry):
        token_grad, prob_grad, sum_gate, sum_up, sum_down = running_sums
        device_index, slots = scan_entry
        live_mask = slots >= 0
        safe_slot = jnp.where(live_mask, slots, 0).astype(jnp.int32)
        token_row = (safe_slot // TOPK).astype(jnp.int32)
        input_rows = jnp.where(live_mask[:, None], tokens[token_row], jnp.zeros((), tokens.dtype))
        grad_rows = jnp.where(live_mask[:, None], grad_out[token_row], jnp.zeros((), grad_out.dtype))
        prob_rows = jnp.where(live_mask, flat_probs[safe_slot], jnp.zeros((), probs.dtype))
        group_index = device_index // columns
        column = device_index % columns
        expert = (column * EXP_DEV + serve_map[group_index, column]).astype(jnp.int32)
        route_grad, route_prob, part_gate, part_up, part_down = expert_backward(
            input_rows, grad_rows, prob_rows, w_gate[expert], w_up[expert], w_down[expert])
        token_target = jnp.where(live_mask, token_row, TOKENS).astype(jnp.int32)
        token_grad = token_grad.at[token_target].add(route_grad.astype(jnp.float32), mode="drop")
        prob_target = jnp.where(live_mask, safe_slot, TOKENS * TOPK).astype(jnp.int32)
        prob_grad = prob_grad.at[prob_target].set(route_prob, mode="drop")
        sum_gate = sum_gate.at[expert].add(part_gate.astype(jnp.float32))
        sum_up = sum_up.at[expert].add(part_up.astype(jnp.float32))
        sum_down = sum_down.at[expert].add(part_down.astype(jnp.float32))
        return (token_grad, prob_grad, sum_gate, sum_up, sum_down), None

    start = (jnp.zeros((TOKENS, D), jnp.float32), jnp.zeros((TOKENS * TOPK,), jnp.bfloat16),
             jnp.zeros((EXPERTS, D, FF_WIN), jnp.float32), jnp.zeros((EXPERTS, D, FF_WIN), jnp.float32),
             jnp.zeros((EXPERTS, D, FF_WIN), jnp.float32))
    final, unused = lax.scan(one_device, start, (jnp.arange(devices, dtype=jnp.int32), slot_table))
    token_grad, prob_grad, sum_gate, sum_up, sum_down = final
    return (token_grad.astype(jnp.bfloat16), prob_grad.reshape(TOKENS, TOPK), sum_gate, sum_up, sum_down)
```

```python
import functools

import jax
import jax.numpy as jnp
from jax import lax
from jax.experimental import pallas as pl
from jax.experimental.pallas import tpu as pltpu
from jax.sharding import PartitionSpec as P

D, F, TOPK, TOK, CAP, GRP, COL = 2048, 768, 6, 128, 8, 8, 16
EXT = D + 128
SEG = GRP * CAP
ROWS = COL * SEG
CHUNK = 4 * SEG
BF, F32 = jnp.bfloat16, jnp.float32
MESH = pl.DeviceIdType.MESH
ANY = pl.BlockSpec(memory_space=pl.ANY)
VM = pl.BlockSpec(memory_space=pltpu.VMEM)

ORDER = [
    (0, 0), (1, 0), (3, 0), (0, 1),
    (0, 3), (1, 1), (3, 1), (1, 3),
    (3, 3), (2, 0), (0, 2), (2, 1),
    (2, 3), (1, 2), (3, 2), (2, 2),
]
SLOT = {place: index for index, place in enumerate(ORDER)}


def here():
    g = lax.axis_index("grp")
    c = lax.axis_index("exp")
    return g, c // 4, c % 4


def near(v, step):
    return lax.rem(v + (step + 4), 4)


class Copies:
    def __init__(self, send, recv):
        self.send, self.recv, self.used, self.sent = send, recv, [], []

    def make(self, src, dst, device):
        i = len(self.used)
        copy = pltpu.make_async_remote_copy(
            src_ref=src, dst_ref=dst, send_sem=self.send.at[i], recv_sem=self.recv.at[i],
            device_id=device, device_id_type=MESH,
        )
        self.used.append(copy)
        return copy

    def go(self, src, dst, device):
        copy = self.make(src, dst, device)
        copy.start()
        return copy

    def wait_send(self, copy):
        self.sent.append(id(copy))
        copy.wait_send()

    def wait_sends(self):
        for copy in self.used:
            if id(copy) not in self.sent:
                copy.wait_send()


def meet(devices):
    barrier = pltpu.get_barrier_semaphore()
    for device in devices:
        pl.semaphore_signal(barrier, inc=1, device_id=device, device_id_type=MESH)
    pl.semaphore_wait(barrier, len(devices))


def matches(routes, dest):
    expert, servers = dest[:, 0:1], dest[:, 1:2]
    place, inverse = dest[:, 2:3], dest[:, 3:4]
    found = []
    for k in range(TOPK):
        pick = routes[8 + k : 9 + k, :]
        turn = pick - jnp.floor((pick + 0.5) * inverse) * servers
        found.append((routes[k : k + 1, :] == expert) & (turn == place))
    return found


def onehot(code):
    spread = jnp.broadcast_to(code[:, None, :], (GRP, CAP, TOK)).reshape(SEG, TOK)
    rank = (lax.broadcasted_iota(jnp.int32, (SEG, TOK), 0) & (CAP - 1)).astype(F32)
    return jnp.where(spread == rank, 1.0, 0.0)


N1 = 96


def dispatch_kernel(
    tok, gout, routes, dest, member, wg_h, wu_h, wd_h,
    x_o, g_o, h_o, dg_o, du_o, rg_o, code_o,
    wg, wu, wd, xb, gb, ty, gz, code, codet, cty, cgz, st, sg, rt, rg_relay,
    hb, dgb, dub, rgb, dgm, dum, send, recv, local,
):
    g, y, z = here()
    at = lambda dy, dz: (g, near(y, dy) * 4 + near(z, dz))
    net = Copies(send, recv)
    nlocal = [0]

    def copy_local(src, dst):
        copy = pltpu.make_async_copy(src, dst, local.at[nlocal[0]])
        nlocal[0] += 1
        copy.start()
        return copy

    weights = [copy_local(h, v) for h, v in ((wg_h, wg), (wd_h, wd), (wu_h, wu))]
    meet([at(1, 0), at(2, 0), at(3, 0), at(0, 1), at(0, 2), at(0, 3)])

    t_fwd = net.go(tok, ty.at[2], at(1, 0))
    g_fwd = net.go(gout, gz.at[2], at(0, 1))
    t_bwd = net.go(tok, ty.at[0], at(3, 0))
    g_bwd = net.go(gout, gz.at[0], at(0, 3))

    routes_v = routes[...]
    found = matches(routes_v, dest[...])
    hit = sum(m.astype(F32) for m in found)
    prob = sum(jnp.where(m, routes_v[16 + k : 17 + k, :], 0.0) for k, m in enumerate(found))
    earlier = (
        lax.broadcasted_iota(jnp.int32, (TOK, TOK), 0)
        < lax.broadcasted_iota(jnp.int32, (TOK, TOK), 1)
    ).astype(F32).astype(BF)
    rank = jnp.dot(hit.astype(BF), earlier, preferred_element_type=F32)
    kept = jnp.where((hit > 0.5) & (rank < CAP - 0.5), rank, -1.0)
    code[:, 0:GRP, :] = kept.reshape(COL, GRP, TOK)
    code[:, GRP:, :] = prob.reshape(COL, GRP, TOK)
    for a in range(4):
        for b in range(4):
            codet[4 * b + a] = code[4 * a + b]
    tables_t, tables_g = [], []
    for s in (1, 2, 3):
        yt, zt = near(y, -s), near(z, -s)
        tables_t.append(net.go(code.at[pl.ds(4 * yt, 4)], cty.at[s - 1], (g, yt * 4 + z)))
        tables_g.append(net.go(codet.at[pl.ds(4 * zt, 4)], cgz.at[s - 1], (g, y * 4 + zt)))
    out_copies = [copy_local(code, code_o)]

    relays = {}
    arrive_t, arrive_g = {}, {}

    def spread_t(dy):
        src = tok if dy == 0 else ty.at[dy - 1]
        if dy:
            tables_t[dy - 1].wait_recv()
        tiles = []
        for dz in range(4):
            zz = near(z, dz)
            tiles.append(code[4 * y + zz, 0:GRP, :] if dy == 0 else cty[dy - 1, zz, 0:GRP, :])
        pick = jnp.concatenate([onehot(t) for t in tiles], axis=0).astype(BF)

        @pl.loop(0, 4)
        def _(n):
            cols = pl.ds(pl.multiple_of(n * 512, 512), 512)
            rows = jnp.dot(pick, src[:, cols], preferred_element_type=F32).astype(BF)
            xb[SEG * SLOT[dy, 0] : SEG * (SLOT[dy, 0] + 1), cols] = rows[0:SEG]
            for dz in (1, 2, 3):
                st[dy * 3 + dz - 1, :, cols] = rows[SEG * dz : SEG * (dz + 1)]

        half = SEG // 2
        far, a, b = st.at[dy * 3 + 1], SEG * SLOT[dy, 2], SEG * SLOT[dy, 2] + half
        one = net.go(far.at[0:half], rt.at[dy], at(0, 1))
        two = net.go(far.at[half:SEG], rt.at[4 + dy], at(0, 3))
        relays["t", dy] = (
            (one, rt.at[dy], xb.at[a : a + half], at(0, 1)),
            (two, rt.at[4 + dy], xb.at[b : b + half], at(0, 3)),
        )
        r = SEG * SLOT[dy, 3]
        arrive_t[dy, 3] = [net.go(st.at[dy * 3], xb.at[r : r + SEG], at(0, 1))]
        r = SEG * SLOT[dy, 1]
        arrive_t[dy, 1] = [net.go(st.at[dy * 3 + 2], xb.at[r : r + SEG], at(0, 3))]

    def spread_g(dz):
        src = gout if dz == 0 else gz.at[dz - 1]
        if dz:
            tables_g[dz - 1].wait_recv()
        picks, extra = [], []
        for dy in range(4):
            yy = near(y, dy)
            table = codet[4 * z + yy] if dz == 0 else cgz[dz - 1, yy]
            hot = onehot(table[0:GRP, :])
            weight = jnp.broadcast_to(table[GRP:, None, :], (GRP, CAP, TOK)).reshape(SEG, TOK)
            picks.append(hot)
            extra.append(
                jnp.broadcast_to(jnp.sum(hot * weight, axis=1, keepdims=True), (SEG, 128)).astype(BF)
            )
        pick = jnp.concatenate(picks, axis=0).astype(BF)
        r0 = SEG * SLOT[0, dz]
        gb[r0 : r0 + SEG, D:EXT] = extra[0]
        for dy in (1, 2, 3):
            sg[dz * 3 + dy - 1, :, D:EXT] = extra[dy]

        @pl.loop(0, 4)
        def _(n):
            cols = pl.ds(pl.multiple_of(n * 512, 512), 512)
            rows = jnp.dot(pick, src[:, cols], preferred_element_type=F32).astype(BF)
            gb[r0 : r0 + SEG, cols] = rows[0:SEG]
            for dy in (1, 2, 3):
                sg[dz * 3 + dy - 1, :, cols] = rows[SEG * dy : SEG * (dy + 1)]

        half = SEG // 2
        far, a, b = sg.at[dz * 3 + 1], SEG * SLOT[2, dz], SEG * SLOT[2, dz] + half
        one = net.go(far.at[0:half], rg_relay.at[dz], at(1, 0))
        two = net.go(far.at[half:SEG], rg_relay.at[4 + dz], at(3, 0))
        relays["g", dz] = (
            (one, rg_relay.at[dz], gb.at[a : a + half], at(1, 0)),
            (two, rg_relay.at[4 + dz], gb.at[b : b + half], at(3, 0)),
        )
        r = SEG * SLOT[3, dz]
        arrive_g[3, dz] = [net.go(sg.at[dz * 3], gb.at[r : r + SEG], at(1, 0))]
        r = SEG * SLOT[1, dz]
        arrive_g[1, dz] = [net.go(sg.at[dz * 3 + 2], gb.at[r : r + SEG], at(3, 0))]

    def pass_on(step):
        for kind, arrive in (("t", arrive_t), ("g", arrive_g)):
            done = []
            for copy, relay, dst, device in relays[kind, step]:
                copy.wait_recv()
                done.append(net.go(relay, dst, device))
            arrive[(step, 2) if kind == "t" else (2, step)] = done

    def compute(ci):
        rows = pl.ds(ci * CHUNK, CHUNK)
        is_one = member[rows, :] > 0.5
        prob_rows = gb[rows, D : D + 1].astype(F32)

        def ff(n, total):
            cols = pl.ds(pl.multiple_of(n * 256, 256), 256)
            x, gr = xb[rows, :], gb[rows, 0:D]

            def both(a, w):
                zero = jnp.dot(a, w[0, :, cols], preferred_element_type=F32)
                one = jnp.dot(a, w[1, :, cols], preferred_element_type=F32)
                return jnp.where(is_one, one, zero)

            gate, up, back = both(x, wg), both(x, wu), both(gr, wd)
            sig = jax.nn.sigmoid(gate)
            silu = gate * sig
            hidden = (silu * up).astype(BF).astype(F32)
            grad = prob_rows * back
            dgate = grad * up * sig * (1.0 + gate * (1.0 - sig))
            dup = grad * silu
            hb[rows, cols] = (prob_rows * hidden).astype(BF)
            dgb[rows, cols] = dgate.astype(BF)
            dub[rows, cols] = dup.astype(BF)
            for e in range(2):
                keep = is_one if e else jnp.logical_not(is_one)
                dgm[e, :, cols] = jnp.where(keep, dgate, 0.0).astype(BF)
                dum[e, :, cols] = jnp.where(keep, dup, 0.0).astype(BF)
            return total + jnp.sum(hidden * back, axis=1, keepdims=True)

        rp = lax.fori_loop(0, F // 256, ff, jnp.zeros((CHUNK, 1), F32))
        rgb[rows, D:EXT] = jnp.broadcast_to(rp, (CHUNK, 128)).astype(BF)
        for src, dst in ((xb, x_o), (hb, h_o), (dgb, dg_o), (dub, du_o)):
            out_copies.append(copy_local(src.at[rows], dst.at[rows]))
        out_copies.append(copy_local(gb.at[rows, 0:D], g_o.at[rows]))

        @pl.loop(0, D // 256)
        def _(n):
            cols = pl.ds(pl.multiple_of(n * 256, 256), 256)
            acc = jnp.zeros((CHUNK, 256), F32)
            for grads, w in ((dgm, wg), (dum, wu)):
                for e in range(2):
                    acc += lax.dot_general(
                        grads[e], w[e, cols, :], (((1,), (1,)), ((), ())),
                        preferred_element_type=F32,
                    )
            rgb[rows, cols] = acc.astype(BF)

        out_copies.append(copy_local(rgb.at[rows], rg_o.at[rows]))

    def arrived(ci):
        for place in ORDER[4 * ci : 4 * ci + 4]:
            for arrive in (arrive_t, arrive_g):
                for copy in arrive.get(place, ()):
                    copy.wait_recv()

    spread_t(0)
    spread_g(0)
    h = TOK // 2
    t_fwd.wait_recv()
    t_far_a = net.go(ty.at[2, 0:h], ty.at[1, 0:h], at(1, 0))
    g_fwd.wait_recv()
    g_far_a = net.go(gz.at[2, 0:h], gz.at[1, 0:h], at(0, 1))
    t_bwd.wait_recv()
    t_far_b = net.go(ty.at[0, h:TOK], ty.at[1, h:TOK], at(3, 0))
    g_bwd.wait_recv()
    g_far_b = net.go(gz.at[0, h:TOK], gz.at[1, h:TOK], at(0, 3))
    spread_t(3)
    spread_g(3)
    spread_t(1)
    spread_g(1)
    pass_on(0)
    for copy in (t_far_a, t_far_b):
        copy.wait_recv()
    spread_t(2)
    for copy in (g_far_a, g_far_b):
        copy.wait_recv()
    spread_g(2)
    pass_on(3)
    pass_on(1)
    for copy in weights:
        copy.wait()
    arrived(0)
    compute(0)
    pass_on(2)
    for ci in (1, 2, 3):
        arrived(ci)
        compute(ci)
    net.wait_sends()
    for copy in out_copies:
        copy.wait()


N2 = 48


def reduce_kernel(
    rg_h, x_h, g_h, h_h, dg_h, du_h, code, routes, dest, member,
    gt_o, gp_o, og, ou, od,
    lx, lg, raw, rm, bp, ocs, ocr, rls, rlr, fs, fr, ret, pall, send, recv, local,
):
    g, y, z = here()
    x, core = g // 2, g % 2
    other = 1 - core
    c = y * 4 + z
    at = lambda dx: (near(x, dx) * 2 + core, c)
    net = Copies(send, recv)
    columns = [(g, near(y, dy) * 4 + near(z, dz)) for dy, dz in ORDER[1:]]
    loads = []
    for i, (src, dst) in enumerate(
        ((g_h, lg), (h_h, raw.at[0]), (x_h, lx), (dg_h, raw.at[1]), (du_h, raw.at[2]))
    ):
        loads.append(pltpu.make_async_copy(src, dst, local.at[i]))
        loads[-1].start()
    own_rows = pltpu.make_async_copy(rg_h.at[0:SEG], ret.at[0:SEG], local.at[5])
    own_rows.start()
    meet([at(1), at(3), (x * 2 + other, c)] + columns)

    back = []
    for (dy, dz), device in list(zip(ORDER[1:], columns))[::-1]:
        r, q = SEG * SLOT[dy, dz], SEG * SLOT[(4 - dy) % 4, (4 - dz) % 4]
        back.append(net.go(rg_h.at[r : r + SEG], ret.at[q : q + SEG], device))

    outs = (od, og, ou)
    left = (lg, lx, lx)
    across, relay_a, relay_b, last_a, last_b = {}, {}, {}, {}, {}

    def mask_rows(m):
        @pl.loop(0, 4)
        def _(i):
            rows = pl.ds(pl.multiple_of(i * 256, 256), 256)
            v = raw[m, rows, :].astype(F32)
            one = member[rows, :] > 0.5
            rm[rows, 0:F] = jnp.where(one, 0.0, v).astype(BF)
            rm[rows, F : 2 * F] = jnp.where(one, v, 0.0).astype(BF)

    def unit(m, i, dx):
        @pl.loop(0, 2)
        def _(j):
            owner = near(x, dx) * 2 + lax.rem(other + j, 2)
            cols = pl.ds(pl.multiple_of(owner * 256, 256), 256)
            bp[i % 2, j] = lax.dot_general(
                left[m][:, cols], rm[...], (((0,), (0,)), ((), ())), preferred_element_type=F32
            )

        if m:
            net.wait_send(across[m - 1, i])
        ocs[i] = bp[i % 2, 0].astype(BF)
        across[m, i] = net.go(ocs.at[i], ocr.at[m * 4 + i], (x * 2 + other, c))

    def combine(m, i, dx):
        across[m, i].wait_recv()
        both = bp[i % 2, 1] + ocr[m * 4 + i].astype(F32)
        if dx == 2:
            rls[2 * m] = both[:, 0:F].astype(BF)
            rls[2 * m + 1] = both[:, F:].astype(BF)
            relay_a[m] = net.go(rls.at[2 * m], rlr.at[2 * m], at(1))
            relay_b[m] = net.go(rls.at[2 * m + 1], rlr.at[2 * m + 1], at(3))
        elif dx == 0:
            outs[m][0] = both[:, 0:F]
            outs[m][1] = both[:, F:]
        else:
            fs[2 * m + (dx == 3)] = both.astype(BF)

    def pass_on(m):
        relay_a[m].wait_recv()
        fs[2 * m, :, 0:F] = (fs[2 * m, :, 0:F].astype(F32) + rlr[2 * m].astype(F32)).astype(BF)
        last_a[m] = net.go(fs.at[2 * m], fr.at[2 * m], at(1))
        relay_b[m].wait_recv()
        fs[2 * m + 1, :, F:] = (
            fs[2 * m + 1, :, F:].astype(F32) + rlr[2 * m + 1].astype(F32)
        ).astype(BF)
        last_b[m] = net.go(fs.at[2 * m + 1], fr.at[2 * m + 1], at(3))

    def finish(m):
        last_a[m].wait_recv()
        last_b[m].wait_recv()
        for e in range(2):
            cols = slice(e * F, (e + 1) * F)
            outs[m][e] += fr[2 * m, :, cols].astype(F32) + fr[2 * m + 1, :, cols].astype(F32)

    loads[0].wait()
    loads[1].wait()
    late = None
    for m in range(3):
        if m == 1:
            loads[2].wait()
            loads[3].wait()
        if m == 2:
            loads[4].wait()
        mask_rows(m)
        for i, dx in enumerate((2, 1, 3, 0)):
            unit(m, i, dx)
            if late is not None:
                combine(*late)
            late = (m, i, dx)
            if m and i == 0:
                pass_on(m - 1)
    combine(*late)
    pass_on(2)

    own_rows.wait()
    for copy in back:
        copy.wait_recv()
    lane = lax.broadcasted_iota(jnp.int32, (SEG, 128), 1)
    group = lax.broadcasted_iota(jnp.int32, (SEG, 128), 0) // CAP
    spread = []
    for s, (dy, dz) in enumerate(ORDER):
        col = near(y, dy) * 4 + near(z, dz)
        pall[s * SEG : (s + 1) * SEG, :] = onehot(code[col, 0:GRP, :]).astype(BF)
        value = ret[s * SEG : (s + 1) * SEG, D:EXT].astype(F32)
        spread.append(jnp.where(lane == group + col * GRP, value, 0.0))
    over_rows = (((0,), (0,)), ((), ()))
    per_dest = lax.dot_general(
        jnp.concatenate(spread, axis=0).astype(BF), pall[...], over_rows, preferred_element_type=F32
    )
    gp_o[...] = jnp.zeros((8, 128), F32)
    for k, m in enumerate(matches(routes[...], dest[...])):
        gp_o[k : k + 1, :] = jnp.sum(jnp.where(m, per_dest, 0.0), axis=0, keepdims=True)

    gt_o[...] = lax.dot_general(
        pall[...], ret[:, 0:D], over_rows, preferred_element_type=F32
    ).astype(BF)
    for m in range(3):
        finish(m)
    net.wait_sends()


def body(tokens, grad_out, probs, expert_ids, serve_map, replica_pick, w_gate, w_up, w_down):
    c = lax.axis_index("exp")
    pad = lambda a: jnp.pad(a.T.astype(F32), ((0, 8 - TOPK), (0, 0)))
    routes = jnp.concatenate([pad(expert_ids), pad(replica_pick), pad(probs)], axis=0)
    served = serve_map.T
    same = served[:, :, None] == served[:, None, :]
    servers = jnp.sum(same, axis=2)
    before = jnp.arange(GRP)[None, None, :] < jnp.arange(GRP)[None, :, None]
    place = jnp.sum(same & before, axis=2)
    expert = jnp.arange(COL)[:, None] * 2 + served
    servers = servers.astype(F32)
    dest = jnp.stack(
        [expert.astype(F32), servers, place.astype(F32), 1.0 / servers], axis=2
    ).reshape(GRP * COL, 4)
    mine = lax.dynamic_index_in_dim(serve_map, c, 1, keepdims=False).astype(F32)
    member = jnp.broadcast_to(mine[None, :, None], (COL, GRP, CAP)).reshape(ROWS, 1)

    wide = lambda n, w, dt=BF: jax.ShapeDtypeStruct((n, w), dt)
    vmem = lambda *s, dt=BF: pltpu.VMEM(s, dt)
    dma = lambda n: pltpu.SemaphoreType.DMA((n,))
    x, gr, h, dg, du, rg, code = pl.pallas_call(
        dispatch_kernel,
        out_shape=[
            wide(ROWS, D), wide(ROWS, D), wide(ROWS, F), wide(ROWS, F), wide(ROWS, F),
            wide(ROWS, EXT), jax.ShapeDtypeStruct((COL, 16, TOK), F32),
        ],
        in_specs=[VM] * 5 + [ANY] * 3,
        out_specs=[ANY] * 7,
        scratch_shapes=[
            vmem(2, D, F), vmem(2, D, F), vmem(2, D, F), vmem(ROWS, D), vmem(ROWS, EXT),
            vmem(3, TOK, D), vmem(3, TOK, D),
            vmem(COL, 16, TOK, dt=F32), vmem(COL, 16, TOK, dt=F32),
            vmem(3, 4, 16, TOK, dt=F32), vmem(3, 4, 16, TOK, dt=F32),
            vmem(12, SEG, D), vmem(12, SEG, EXT),
            vmem(8, SEG // 2, D), vmem(8, SEG // 2, EXT),
            vmem(ROWS, F), vmem(ROWS, F), vmem(ROWS, F), vmem(ROWS, EXT),
            vmem(2, CHUNK, F), vmem(2, CHUNK, F),
            dma(N1), dma(N1), dma(32),
        ],
        compiler_params=pltpu.CompilerParams(
            collective_id=0, has_side_effects=True, vmem_limit_bytes=60 * 2**20
        ),
        name="dispatch",
    )(tokens, grad_out, routes, dest, member, w_gate, w_up, w_down)

    out = jax.ShapeDtypeStruct((2, 256, F), F32)
    gt, gp, og, ou, od = pl.pallas_call(
        reduce_kernel,
        out_shape=[wide(TOK, D), wide(8, TOK, F32), out, out, out],
        in_specs=[ANY] * 6 + [VM] * 4,
        out_specs=[VM] * 5,
        scratch_shapes=[
            vmem(ROWS, D), vmem(ROWS, D), vmem(3, ROWS, F), vmem(ROWS, 2 * F),
            vmem(2, 2, 256, 2 * F, dt=F32),
            vmem(4, 256, 2 * F), vmem(12, 256, 2 * F),
            vmem(6, 256, F), vmem(6, 256, F), vmem(6, 256, 2 * F), vmem(6, 256, 2 * F),
            vmem(ROWS, EXT), vmem(ROWS, TOK), dma(N2), dma(N2), dma(8),
        ],
        compiler_params=pltpu.CompilerParams(
            collective_id=1, has_side_effects=True, vmem_limit_bytes=64 * 2**20
        ),
        name="reduce",
    )(rg, x, gr, h, dg, du, code, routes, dest, member)
    return (gt, gp[:TOPK].T.astype(BF), og, ou, od)


def solution(mesh):
    rows = P(("grp", "exp"), None)
    by_expert = P("exp", None, None)
    return jax.shard_map(
        body,
        mesh=mesh,
        in_specs=(rows, rows, rows, rows, P(), rows, by_expert, by_expert, by_expert),
        out_specs=(rows, rows) + (P("exp", "grp", None),) * 3,
        check_vma=False,
    )
```

```python
import functools

import jax
import jax.numpy as jnp
from jax import lax
from jax.experimental import pallas as pl
from jax.experimental.pallas import tpu as pltpu
from jax.sharding import PartitionSpec as P

D, F, TOPK, TOK, CAP, GRP, COL = 2048, 768, 6, 128, 8, 8, 16
EXT = D + 128
SEG = GRP * CAP
ROWS = COL * SEG
CHUNK = 4 * SEG
BF, F32 = jnp.bfloat16, jnp.float32
MESH = pl.DeviceIdType.MESH
ANY = pl.BlockSpec(memory_space=pl.ANY)
VM = pl.BlockSpec(memory_space=pltpu.VMEM)

ORDER = [
    (0, 0), (1, 0), (3, 0), (0, 1),
    (0, 3), (1, 1), (3, 1), (1, 3),
    (3, 3), (2, 0), (0, 2), (2, 1),
    (2, 3), (1, 2), (3, 2), (2, 2),
]
SLOT = {place: index for index, place in enumerate(ORDER)}


def here():
    g = lax.axis_index("grp")
    c = lax.axis_index("exp")
    return g, c // 4, c % 4


def near(v, step):
    return lax.rem(v + (step + 4), 4)


class Copies:
    def __init__(self, send, recv):
        self.send, self.recv, self.used, self.sent = send, recv, [], []

    def make(self, src, dst, device):
        i = len(self.used)
        copy = pltpu.make_async_remote_copy(
            src_ref=src, dst_ref=dst, send_sem=self.send.at[i], recv_sem=self.recv.at[i],
            device_id=device, device_id_type=MESH,
        )
        self.used.append(copy)
        return copy

    def go(self, src, dst, device):
        copy = self.make(src, dst, device)
        copy.start()
        return copy

    def wait_send(self, copy):
        self.sent.append(id(copy))
        copy.wait_send()

    def wait_sends(self, but=()):
        later = [id(copy) for copy in but]
        for copy in self.used:
            if id(copy) not in self.sent and id(copy) not in later:
                self.wait_send(copy)


def meet(devices):
    barrier = pltpu.get_barrier_semaphore()
    for device in devices:
        pl.semaphore_signal(barrier, inc=1, device_id=device, device_id_type=MESH)
    pl.semaphore_wait(barrier, len(devices))


def destinations(serve):
    dest = lax.broadcasted_iota(jnp.int32, (GRP * COL, COL), 0) // GRP
    of_column = (dest == lax.broadcasted_iota(jnp.int32, (GRP * COL, COL), 1)).astype(F32)
    peers = lax.dot_general(
        of_column.astype(BF), serve.astype(F32).astype(BF), (((1,), (1,)), ((), ())),
        preferred_element_type=F32,
    )
    lane = lax.broadcasted_iota(jnp.int32, (GRP * COL, GRP), 1)
    row = lax.broadcasted_iota(jnp.int32, (GRP * COL, GRP), 0)
    group = row % GRP
    served = jnp.sum(jnp.where(lane == group, peers, 0.0), axis=1, keepdims=True)
    same = jnp.where(peers == served, 1.0, 0.0)
    servers = jnp.sum(same, axis=1, keepdims=True)
    place = jnp.sum(jnp.where(lane < group, same, 0.0), axis=1, keepdims=True)
    expert = 2.0 * (row[:, 0:1] // GRP).astype(F32) + served
    return expert, servers, place


def onehot(code):
    spread = jnp.broadcast_to(code[:, None, :], (GRP, CAP, TOK)).reshape(SEG, TOK)
    rank = (lax.broadcasted_iota(jnp.int32, (SEG, TOK), 0) & (CAP - 1)).astype(F32)
    return jnp.where(spread == rank, 1.0, 0.0)


NCOPY = 144


def layer_kernel(
    tok, gout, ids, picks, probs, serve, wg_h, wu_h, wd_h,
    gp_o, gt_o, og, ou, od, ret_h,
    wg, wu, wd, xb, gb, ty, gz, code, codet, cty, cgz, st, sg, rt, rg_relay,
    hb, dgb, dub, rpb, retp, member, destk, ocr, rlr, send, recv, local,
):
    g, y, z = here()
    x, core = g // 2, g % 2
    other = 1 - core
    c = y * 4 + z
    at = lambda dy, dz: (g, near(y, dy) * 4 + near(z, dz))
    along = lambda dx: (near(x, dx) * 2 + core, c)
    net = Copies(send, recv)
    columns = [at(dy, dz) for dy, dz in ORDER]
    nlocal = [0]

    def copy_local(src, dst):
        copy = pltpu.make_async_copy(src, dst, local.at[nlocal[0]])
        nlocal[0] += 1
        copy.start()
        return copy

    weights = [copy_local(wg_h, wg), copy_local(wu_h, wu)]
    for e in range(2):
        for i in range(8):
            weights.append(copy_local(wd_h.at[e, 256 * i : 256 * (i + 1)], wd.at[8 * e + i]))
    meet(columns[1:] + [along(1), along(3), (x * 2 + other, c)])

    t_fwd = net.go(tok, ty.at[2], at(1, 0))
    g_fwd = net.go(gout, gz.at[2], at(0, 1))
    t_bwd = net.go(tok, ty.at[0], at(3, 0))
    g_bwd = net.go(gout, gz.at[0], at(0, 3))

    expert, servers, place = destinations(serve[...])
    inverse = 1.0 / servers
    ids_v, picks_v, probs_v = ids[...].astype(F32), picks[...].astype(F32), probs[...].astype(F32)
    number = lax.broadcasted_iota(jnp.int32, (GRP * COL, TOK), 0).astype(F32)
    hit, prob = jnp.zeros((GRP * COL, TOK), F32), jnp.zeros((GRP * COL, TOK), F32)
    destk[...] = jnp.zeros((8, TOK), F32)
    for k in range(TOPK):
        pick = picks_v[k : k + 1, :]
        turn = pick - jnp.floor((pick + 0.5) * inverse) * servers
        match = (ids_v[k : k + 1, :] == expert) & (turn == place)
        hit += jnp.where(match, 1.0, 0.0)
        prob += jnp.where(match, probs_v[k : k + 1, :], 0.0)
        destk[k : k + 1, :] = jnp.sum(jnp.where(match, number, 0.0), axis=0, keepdims=True)
    earlier = (
        lax.broadcasted_iota(jnp.int32, (TOK, TOK), 0)
        < lax.broadcasted_iota(jnp.int32, (TOK, TOK), 1)
    ).astype(F32).astype(BF)
    rank = jnp.dot(hit.astype(BF), earlier, preferred_element_type=F32)
    kept = jnp.where((hit > 0.5) & (rank < CAP - 0.5), rank, -1.0)
    code[:, 0:GRP, :] = kept.reshape(COL, GRP, TOK)
    code[:, GRP:, :] = prob.reshape(COL, GRP, TOK)
    for a in range(4):
        for b in range(4):
            codet[4 * b + a] = code[4 * a + b]
    tables_t, tables_g = [], []
    for s in (1, 2, 3):
        yt, zt = near(y, -s), near(z, -s)
        tables_t.append(net.go(code.at[pl.ds(4 * yt, 4)], cty.at[s - 1], (g, yt * 4 + z)))
        tables_g.append(net.go(codet.at[pl.ds(4 * zt, 4)], cgz.at[s - 1], (g, y * 4 + zt)))
    here_serve = lax.broadcasted_iota(jnp.int32, (GRP, COL), 1) == y * 4 + z
    mine = jnp.sum(jnp.where(here_serve, serve[...], 0).astype(F32), axis=1, keepdims=True)
    per_row = jnp.broadcast_to(mine[:, None, :], (GRP, CAP, 1)).reshape(SEG, 1)
    for i in range(CHUNK // SEG):
        member[SEG * i : SEG * (i + 1), :] = per_row

    relays = {}
    arrive_t, arrive_g = {}, {}

    def spread_t(dy):
        src = tok if dy == 0 else ty.at[dy - 1]
        if dy:
            tables_t[dy - 1].wait_recv()
        tiles = []
        for dz in range(4):
            zz = near(z, dz)
            tiles.append(code[4 * y + zz, 0:GRP, :] if dy == 0 else cty[dy - 1, zz, 0:GRP, :])
        pick = jnp.concatenate([onehot(t) for t in tiles], axis=0).astype(BF)

        @pl.loop(0, 4)
        def _(n):
            cols = pl.ds(pl.multiple_of(n * 512, 512), 512)
            rows = jnp.dot(pick, src[:, cols], preferred_element_type=F32).astype(BF)
            xb[SEG * SLOT[dy, 0] : SEG * (SLOT[dy, 0] + 1), cols] = rows[0:SEG]
            for dz in (1, 2, 3):
                st[dy * 3 + dz - 1, :, cols] = rows[SEG * dz : SEG * (dz + 1)]

    def send_far_t(dy):
        half = SEG // 2
        far, a, b = st.at[dy * 3 + 1], SEG * SLOT[dy, 2], SEG * SLOT[dy, 2] + half
        one = net.go(far.at[0:half], rt.at[dy], at(0, 1))
        two = net.go(far.at[half:SEG], rt.at[4 + dy], at(0, 3))
        relays["t", dy] = (
            (one, rt.at[dy], xb.at[a : a + half], at(0, 1)),
            (two, rt.at[4 + dy], xb.at[b : b + half], at(0, 3)),
        )

    def send_near_t(dy):
        r = SEG * SLOT[dy, 3]
        arrive_t[dy, 3] = [net.go(st.at[dy * 3], xb.at[r : r + SEG], at(0, 1))]
        r = SEG * SLOT[dy, 1]
        arrive_t[dy, 1] = [net.go(st.at[dy * 3 + 2], xb.at[r : r + SEG], at(0, 3))]

    def spread_g(dz):
        src = gout if dz == 0 else gz.at[dz - 1]
        if dz:
            tables_g[dz - 1].wait_recv()
        picks, extra = [], []
        for dy in range(4):
            yy = near(y, dy)
            table = codet[4 * z + yy] if dz == 0 else cgz[dz - 1, yy]
            hot = onehot(table[0:GRP, :])
            weight = jnp.broadcast_to(table[GRP:, None, :], (GRP, CAP, TOK)).reshape(SEG, TOK)
            picks.append(hot)
            extra.append(
                jnp.broadcast_to(jnp.sum(hot * weight, axis=1, keepdims=True), (SEG, 128)).astype(BF)
            )
        pick = jnp.concatenate(picks, axis=0).astype(BF)
        r0 = SEG * SLOT[0, dz]
        gb[r0 : r0 + SEG, D:EXT] = extra[0]
        for dy in (1, 2, 3):
            sg[dz * 3 + dy - 1, :, D:EXT] = extra[dy]

        @pl.loop(0, 4)
        def _(n):
            cols = pl.ds(pl.multiple_of(n * 512, 512), 512)
            rows = jnp.dot(pick, src[:, cols], preferred_element_type=F32).astype(BF)
            gb[r0 : r0 + SEG, cols] = rows[0:SEG]
            for dy in (1, 2, 3):
                sg[dz * 3 + dy - 1, :, cols] = rows[SEG * dy : SEG * (dy + 1)]

    def send_far_g(dz):
        half = SEG // 2
        far, a, b = sg.at[dz * 3 + 1], SEG * SLOT[2, dz], SEG * SLOT[2, dz] + half
        one = net.go(far.at[0:half], rg_relay.at[dz], at(1, 0))
        two = net.go(far.at[half:SEG], rg_relay.at[4 + dz], at(3, 0))
        relays["g", dz] = (
            (one, rg_relay.at[dz], gb.at[a : a + half], at(1, 0)),
            (two, rg_relay.at[4 + dz], gb.at[b : b + half], at(3, 0)),
        )

    def send_near_g(dz):
        r = SEG * SLOT[3, dz]
        arrive_g[3, dz] = [net.go(sg.at[dz * 3], gb.at[r : r + SEG], at(1, 0))]
        r = SEG * SLOT[1, dz]
        arrive_g[1, dz] = [net.go(sg.at[dz * 3 + 2], gb.at[r : r + SEG], at(3, 0))]

    def send_near(step):
        send_near_t(step)
        send_near_g(step)

    def pass_on(step):
        for kind, arrive in (("t", arrive_t), ("g", arrive_g)):
            done = []
            for copy, relay, dst, device in relays[kind, step]:
                copy.wait_recv()
                done.append(net.go(relay, dst, device))
            arrive[(step, 2) if kind == "t" else (2, step)] = done

    def compute(ci):
        rows = pl.ds(ci * CHUNK, CHUNK)
        is_one = member[...] > 0.5
        prob_rows = gb[rows, D : D + 1].astype(F32)

        def ff(n, total):
            start = pl.multiple_of(n * 256, 256)
            cols = pl.ds(start, 256)
            rows_x, gr = xb[rows, :], gb[rows, 0:D]

            def both(a, w):
                zero = jnp.dot(a, w[0], preferred_element_type=F32)
                one = jnp.dot(a, w[1], preferred_element_type=F32)
                return jnp.where(is_one, one, zero)

            down = [wd[8 * e : 8 * e + 8, :, cols].reshape(D, 256) for e in range(2)]
            gate = both(rows_x, [wg[e, :, cols] for e in range(2)])
            up = both(rows_x, [wu[e, :, cols] for e in range(2)])
            back = both(gr, down)
            sig = jax.nn.sigmoid(gate)
            silu = gate * sig
            hidden = (silu * up).astype(BF).astype(F32)
            grad = prob_rows * back
            dgate = grad * up * sig * (1.0 + gate * (1.0 - sig))
            for out, value in ((hb, prob_rows * hidden), (dgb, dgate), (dub, grad * silu)):
                out[rows, cols] = jnp.where(is_one, 0.0, value).astype(BF)
                out[rows, pl.ds(pl.multiple_of(start + F, 256), 256)] = jnp.where(
                    is_one, value, 0.0
                ).astype(BF)
            return total + jnp.sum(hidden * back, axis=1, keepdims=True)

        rp = lax.fori_loop(0, F // 256, ff, jnp.zeros((CHUNK, 1), F32))
        rpb[rows, :] = jnp.broadcast_to(rp, (CHUNK, 128)).astype(BF)

    def row_grads(ci, out):
        rows = pl.ds(ci * CHUNK, CHUNK)

        @pl.loop(0, D // 256)
        def _(n):
            cols = pl.ds(pl.multiple_of(n * 256, 256), 256)
            acc = jnp.zeros((CHUNK, 256), F32)
            for grads, w in ((dgb, wg), (dub, wu)):
                for e in range(2):
                    acc += lax.dot_general(
                        grads[rows, e * F : (e + 1) * F], w[e, cols, :], (((1,), (1,)), ((), ())),
                        preferred_element_type=F32,
                    )
            acc = acc.astype(BF)
            for i, part in enumerate(out):
                size = CHUNK // len(out)
                part[:, cols] = acc[size * i : size * (i + 1)]

    def arrived(ci):
        for place in ORDER[4 * ci : 4 * ci + 4]:
            for arrive in (arrive_t, arrive_g):
                for copy in arrive.get(place, ()):
                    copy.wait_recv()

    returns = []

    def give_back(ci, out):
        per = CHUNK // len(out) // SEG
        for j in range(3, -1, -1):
            i = 4 * ci + j
            dy, dz = ORDER[i]
            q = SEG * SLOT[(4 - dy) % 4, (4 - dz) % 4]
            here_rows = out[j // per].at[SEG * (j % per) : SEG * (j % per + 1)]
            factor = rpb.at[SEG * i : SEG * (i + 1)]
            if i == 0:
                returns.append(copy_local(here_rows, ret_h.at[0:SEG]))
                returns.append(copy_local(factor, retp.at[0:SEG]))
            else:
                pieces.append(net.go(here_rows, ret_h.at[q : q + SEG], columns[i]))
                pieces.append(net.go(factor, retp.at[q : q + SEG], columns[i]))

    pieces = []
    first, second = [ty.at[0], ty.at[1]], [gz.at[0], gz.at[1]]

    def dispatch():
        spread_t(0)
        spread_g(0)
        h = TOK // 2
        t_fwd.wait_recv()
        t_far_a = net.go(ty.at[2, 0:h], ty.at[1, 0:h], at(1, 0))
        g_fwd.wait_recv()
        g_far_a = net.go(gz.at[2, 0:h], gz.at[1, 0:h], at(0, 1))
        t_bwd.wait_recv()
        t_far_b = net.go(ty.at[0, h:TOK], ty.at[1, h:TOK], at(3, 0))
        g_bwd.wait_recv()
        g_far_b = net.go(gz.at[0, h:TOK], gz.at[1, h:TOK], at(0, 3))
        send_far_t(0)
        send_far_g(0)
        send_near(0)
        for step in (3, 1):
            spread_t(step)
            send_far_t(step)
            spread_g(step)
            send_far_g(step)
        for copy in (t_far_a, t_far_b):
            copy.wait_recv()
        spread_t(2)
        send_far_t(2)
        for copy in (g_far_a, g_far_b):
            copy.wait_recv()
        spread_g(2)
        send_far_g(2)
        send_near(3)
        pass_on(0)
        send_near(1)
        pass_on(3)
        send_near(2)
        for copy in weights:
            copy.wait()
        for copy in (t_far_a, t_far_b, g_far_a, g_far_b):
            net.wait_send(copy)
        arrived(0)
        compute(0)
        pass_on(1)
        pass_on(2)
        row_grads(0, first)
        arrived(1)
        compute(1)
        row_grads(1, second)
        arrived(2)
        compute(2)
        arrived(3)
        give_back(0, first)
        give_back(1, second)
        compute(3)
        net.wait_sends(but=pieces)

    dispatch()

    outs = (od, og, ou)
    left, right = (gb, xb, xb), (hb, dgb, dub)
    across, relay_a, relay_b, last_a, last_b = {}, {}, {}, {}, {}
    writes = []

    def reduce():
        def unit(m, dx):
            turn = len(across)
            theirs = wd.at[12 + 2 * (turn % 2) : 14 + 2 * (turn % 2)]

            def part(side):
                owner = near(x, dx) * 2 + side
                cols = pl.ds(pl.multiple_of(owner * 256, 256), 256)
                return lax.dot_general(
                    left[m][:, cols], right[m][...], (((0,), (0,)), ((), ())),
                    preferred_element_type=F32,
                )

            if turn >= 2:
                net.wait_send(list(across.values())[turn - 2])
            value = part(other)
            theirs[0] = value[:, 0:F].astype(BF)
            theirs[1] = value[:, F:].astype(BF)
            across[m, dx] = net.go(theirs, ocr.at[4 * m + dx], (x * 2 + other, c))
            value = part(core)
            across[m, dx].wait_recv()
            both = ocr.at[4 * m + dx]
            both[0] = (value[:, 0:F] + both[0].astype(F32)).astype(BF)
            both[1] = (value[:, F:] + both[1].astype(F32)).astype(BF)
            if dx == 2:
                relay_a[m] = net.go(both.at[0], rlr.at[2 * m], along(1))
                relay_b[m] = net.go(both.at[1], rlr.at[2 * m + 1], along(3))

        def fold(m):
            relay_a[m].wait_recv()
            relay_b[m].wait_recv()
            a, b = ocr.at[4 * m + 1], ocr.at[4 * m + 3]
            a[0] = (a[0].astype(F32) + rlr[2 * m].astype(F32)).astype(BF)
            last_a[m] = net.go(a, wd.at[4 * m : 4 * m + 2], along(1))
            b[1] = (b[1].astype(F32) + rlr[2 * m + 1].astype(F32)).astype(BF)
            last_b[m] = net.go(b, wd.at[4 * m + 2 : 4 * m + 4], along(3))

        def finish(m):
            last_a[m].wait_recv()
            last_b[m].wait_recv()
            mine = ocr.at[4 * m]
            mine[...] = (
                mine[...].astype(F32)
                + wd[4 * m : 4 * m + 2].astype(F32)
                + wd[4 * m + 2 : 4 * m + 4].astype(F32)
            ).astype(BF)
            writes.append(copy_local(mine, outs[m]))

        third, fourth = [st.at[i] for i in range(4)], [st.at[4 + i] for i in range(4)]
        for do in PLAN:
            if do[0] == "p":
                fold(int(do[1]))
            elif do == "r2":
                row_grads(2, third)
                give_back(2, third)
            elif do == "r3":
                row_grads(3, fourth)
                give_back(3, fourth)
            else:
                unit(int(do[0]), int(do[1]))
        fold(2)

        for copy in returns:
            copy.wait()
        for copy in pieces:
            copy.wait_recv()
        back = copy_local(ret_h, gb.at[:, 0:D])
        for copy in pieces:
            net.wait_send(copy)
        pall = rpb
        lane = lax.broadcasted_iota(jnp.int32, (SEG, 128), 1)
        group = lax.broadcasted_iota(jnp.int32, (SEG, 128), 0) // CAP
        spread = []
        for s, (dy, dz) in enumerate(ORDER):
            col = near(y, dy) * 4 + near(z, dz)
            pall[s * SEG : (s + 1) * SEG, :] = onehot(code[col, 0:GRP, :]).astype(BF)
            value = retp[s * SEG : (s + 1) * SEG, :].astype(F32)
            spread.append(jnp.where(lane == group + col * GRP, value, 0.0))
        over_rows = (((0,), (0,)), ((), ()))
        per_dest = lax.dot_general(
            jnp.concatenate(spread, axis=0).astype(BF), pall[...], over_rows,
            preferred_element_type=F32,
        )
        number = lax.broadcasted_iota(jnp.int32, (GRP * COL, TOK), 0).astype(F32)
        for k in range(TOPK):
            mine = jnp.where(number == destk[k : k + 1, :], per_dest, 0.0)
            gp_o[k : k + 1, :] = jnp.sum(mine, axis=0, keepdims=True).astype(BF)
        back.wait()
        total = lax.dot_general(
            pall[...], gb[:, 0:D], over_rows, preferred_element_type=F32
        ).astype(BF)
        for i in range(4):
            rt[i] = total[32 * i : 32 * (i + 1)]
            writes.append(copy_local(rt.at[i], gt_o.at[32 * i : 32 * (i + 1)]))
        for m in range(3):
            finish(m)
        net.wait_sends()
        for copy in writes:
            copy.wait()

    reduce()


PLAN = ["02", "01", "03", "12", "p0", "r2", "11", "13", "r3", "22", "p1", "00", "10", "21", "23", "20"]


def body(tokens, grad_out, probs, expert_ids, serve_map, replica_pick, w_gate, w_up, w_down):
    wide = lambda n, w, dt=BF: jax.ShapeDtypeStruct((n, w), dt)
    vmem = lambda *s, dt=BF: pltpu.VMEM(s, dt)
    dma = lambda n: pltpu.SemaphoreType.DMA((n,))
    out = jax.ShapeDtypeStruct((2, 256, F), BF)
    gp, gt, og, ou, od, _ = pl.pallas_call(
        layer_kernel,
        out_shape=[wide(TOPK, TOK), wide(TOK, D), out, out, out, wide(ROWS, D)],
        in_specs=[VM] * 6 + [ANY] * 3,
        out_specs=[VM] + [ANY] * 5,
        scratch_shapes=[
            vmem(2, D, F), vmem(2, D, F), vmem(16, 256, F), vmem(ROWS, D), vmem(ROWS, EXT),
            vmem(3, TOK, D), vmem(3, TOK, D),
            vmem(COL, 16, TOK, dt=F32), vmem(COL, 16, TOK, dt=F32),
            vmem(3, 4, 16, TOK, dt=F32), vmem(3, 4, 16, TOK, dt=F32),
            vmem(12, SEG, D), vmem(12, SEG, EXT), vmem(8, SEG // 2, D), vmem(8, SEG // 2, EXT),
            vmem(ROWS, 2 * F), vmem(ROWS, 2 * F), vmem(ROWS, 2 * F), vmem(ROWS, 128), vmem(ROWS, 128),
            vmem(CHUNK, 1, dt=F32), vmem(8, TOK, dt=F32),
            vmem(12, 2, 256, F), vmem(6, 256, F),
            dma(NCOPY), dma(NCOPY), dma(40),
        ],
        compiler_params=pltpu.CompilerParams(
            collective_id=0, has_side_effects=True, vmem_limit_bytes=64 * 2**20
        ),
        name="layer",
    )(tokens, grad_out, expert_ids.T, replica_pick.T, probs.T, serve_map, w_gate, w_up, w_down)
    return (gt, gp.T, og.astype(F32), ou.astype(F32), od.astype(F32))


def solution(mesh):
    rows = P(("grp", "exp"), None)
    by_expert = P("exp", None, None)
    return jax.shard_map(
        body,
        mesh=mesh,
        in_specs=(rows, rows, rows, rows, P(), rows, by_expert, by_expert, by_expert),
        out_specs=(rows, rows) + (P("exp", "grp", None),) * 3,
        check_vma=False,
    )
```

```python
import functools

import jax
import jax.numpy as jnp
from jax import lax
from jax.experimental import pallas as pl
from jax.experimental.pallas import tpu as pltpu
from jax.sharding import PartitionSpec as P

D, F, TOPK, TOK, CAP, GRP, COL = 2048, 768, 6, 128, 8, 8, 16
EXT = D + 128
SEG = GRP * CAP
ROWS = COL * SEG
CHUNK = 4 * SEG
BF, F32 = jnp.bfloat16, jnp.float32
MESH = pl.DeviceIdType.MESH
ANY = pl.BlockSpec(memory_space=pl.ANY)
VM = pl.BlockSpec(memory_space=pltpu.VMEM)

ORDER = [
    (0, 0), (1, 0), (3, 0), (0, 1),
    (0, 3), (1, 1), (3, 1), (1, 3),
    (3, 3), (2, 0), (0, 2), (2, 1),
    (2, 3), (1, 2), (3, 2), (2, 2),
]
SLOT = {place: index for index, place in enumerate(ORDER)}


def here():
    g = lax.axis_index("grp")
    c = lax.axis_index("exp")
    return g, c // 4, c % 4


def near(v, step):
    return lax.rem(v + (step + 4), 4)


class Copies:
    def __init__(self, send, recv):
        self.send, self.recv, self.used, self.sent = send, recv, [], []

    def make(self, src, dst, device):
        i = len(self.used)
        copy = pltpu.make_async_remote_copy(
            src_ref=src, dst_ref=dst, send_sem=self.send.at[i], recv_sem=self.recv.at[i],
            device_id=device, device_id_type=MESH,
        )
        self.used.append(copy)
        return copy

    def go(self, src, dst, device):
        copy = self.make(src, dst, device)
        copy.start()
        return copy

    def wait_send(self, copy):
        self.sent.append(id(copy))
        copy.wait_send()

    def wait_sends(self, but=()):
        later = [id(copy) for copy in but]
        for copy in self.used:
            if id(copy) not in self.sent and id(copy) not in later:
                self.wait_send(copy)


def meet(devices):
    barrier = pltpu.get_barrier_semaphore()
    for device in devices:
        pl.semaphore_signal(barrier, inc=1, device_id=device, device_id_type=MESH)
    pl.semaphore_wait(barrier, len(devices))


def destinations(serve):
    dest = lax.broadcasted_iota(jnp.int32, (GRP * COL, COL), 0) // GRP
    of_column = (dest == lax.broadcasted_iota(jnp.int32, (GRP * COL, COL), 1)).astype(F32)
    peers = lax.dot_general(
        of_column.astype(BF), serve.astype(F32).astype(BF), (((1,), (1,)), ((), ())),
        preferred_element_type=F32,
    )
    lane = lax.broadcasted_iota(jnp.int32, (GRP * COL, GRP), 1)
    row = lax.broadcasted_iota(jnp.int32, (GRP * COL, GRP), 0)
    group = row % GRP
    served = jnp.sum(jnp.where(lane == group, peers, 0.0), axis=1, keepdims=True)
    same = jnp.where(peers == served, 1.0, 0.0)
    servers = jnp.sum(same, axis=1, keepdims=True)
    place = jnp.sum(jnp.where(lane < group, same, 0.0), axis=1, keepdims=True)
    expert = 2.0 * (row[:, 0:1] // GRP).astype(F32) + served
    return expert, servers, place


def onehot(code):
    spread = jnp.broadcast_to(code[:, None, :], (GRP, CAP, TOK)).reshape(SEG, TOK)
    rank = (lax.broadcasted_iota(jnp.int32, (SEG, TOK), 0) & (CAP - 1)).astype(F32)
    return jnp.where(spread == rank, 1.0, 0.0)


NCOPY = 144


def layer_kernel(
    tok, gout, ids, picks, probs, serve, wg_h, wu_h, wd_h,
    gp_o, gt_o, og, ou, od, ret_h,
    wg, wu, wd, xb, gb, ty, gz, code, codet, cty, cgz, st, sg, rt, rg_relay,
    hb, dgb, dub, rpb, retp, member, destk, ocr, rlr, send, recv, local,
):
    g, y, z = here()
    x, core = g // 2, g % 2
    other = 1 - core
    c = y * 4 + z
    at = lambda dy, dz: (g, near(y, dy) * 4 + near(z, dz))
    along = lambda dx: (near(x, dx) * 2 + core, c)
    net = Copies(send, recv)
    columns = [at(dy, dz) for dy, dz in ORDER]
    nlocal = [0]

    def copy_local(src, dst):
        copy = pltpu.make_async_copy(src, dst, local.at[nlocal[0]])
        nlocal[0] += 1
        copy.start()
        return copy

    weights = [copy_local(wg_h, wg), copy_local(wu_h, wu)]
    for e in range(2):
        for i in range(8):
            weights.append(copy_local(wd_h.at[e, 256 * i : 256 * (i + 1)], wd.at[8 * e + i]))
    meet(columns[1:] + [along(1), along(3), (x * 2 + other, c)])

    t_fwd = net.go(tok, ty.at[2], at(1, 0))
    g_fwd = net.go(gout, gz.at[2], at(0, 1))
    t_bwd = net.go(tok, ty.at[0], at(3, 0))
    g_bwd = net.go(gout, gz.at[0], at(0, 3))

    expert, servers, place = destinations(serve[...])
    inverse = 1.0 / servers
    ids_v, picks_v, probs_v = ids[...].astype(F32), picks[...].astype(F32), probs[...].astype(F32)
    number = lax.broadcasted_iota(jnp.int32, (GRP * COL, TOK), 0).astype(F32)
    hit, prob = jnp.zeros((GRP * COL, TOK), F32), jnp.zeros((GRP * COL, TOK), F32)
    destk[...] = jnp.zeros((8, TOK), F32)
    for k in range(TOPK):
        pick = picks_v[k : k + 1, :]
        turn = pick - jnp.floor((pick + 0.5) * inverse) * servers
        match = (ids_v[k : k + 1, :] == expert) & (turn == place)
        hit += jnp.where(match, 1.0, 0.0)
        prob += jnp.where(match, probs_v[k : k + 1, :], 0.0)
        destk[k : k + 1, :] = jnp.sum(jnp.where(match, number, 0.0), axis=0, keepdims=True)
    earlier = (
        lax.broadcasted_iota(jnp.int32, (TOK, TOK), 0)
        < lax.broadcasted_iota(jnp.int32, (TOK, TOK), 1)
    ).astype(F32).astype(BF)
    rank = jnp.dot(hit.astype(BF), earlier, preferred_element_type=F32)
    kept = jnp.where((hit > 0.5) & (rank < CAP - 0.5), rank, -1.0)
    code[:, 0:GRP, :] = kept.reshape(COL, GRP, TOK)
    code[:, GRP:, :] = prob.reshape(COL, GRP, TOK)
    for a in range(4):
        for b in range(4):
            codet[4 * b + a] = code[4 * a + b]
    tables_t, tables_g = [], []
    for s in (1, 2, 3):
        yt, zt = near(y, -s), near(z, -s)
        tables_t.append(net.go(code.at[pl.ds(4 * yt, 4)], cty.at[s - 1], (g, yt * 4 + z)))
        tables_g.append(net.go(codet.at[pl.ds(4 * zt, 4)], cgz.at[s - 1], (g, y * 4 + zt)))
    here_serve = lax.broadcasted_iota(jnp.int32, (GRP, COL), 1) == y * 4 + z
    mine = jnp.sum(jnp.where(here_serve, serve[...], 0).astype(F32), axis=1, keepdims=True)
    per_row = jnp.broadcast_to(mine[:, None, :], (GRP, CAP, 1)).reshape(SEG, 1)
    for i in range(CHUNK // SEG):
        member[SEG * i : SEG * (i + 1), :] = per_row

    relays = {}
    arrive_t, arrive_g = {}, {}

    def spread_t(dy):
        src = tok if dy == 0 else ty.at[dy - 1]
        if dy:
            tables_t[dy - 1].wait_recv()
        tiles = []
        for dz in range(4):
            zz = near(z, dz)
            tiles.append(code[4 * y + zz, 0:GRP, :] if dy == 0 else cty[dy - 1, zz, 0:GRP, :])
        pick = jnp.concatenate([onehot(t) for t in tiles], axis=0).astype(BF)

        @pl.loop(0, 4)
        def _(n):
            cols = pl.ds(pl.multiple_of(n * 512, 512), 512)
            rows = jnp.dot(pick, src[:, cols], preferred_element_type=F32).astype(BF)
            xb[SEG * SLOT[dy, 0] : SEG * (SLOT[dy, 0] + 1), cols] = rows[0:SEG]
            for dz in (1, 2, 3):
                st[dy * 3 + dz - 1, :, cols] = rows[SEG * dz : SEG * (dz + 1)]

    def send_far_t(dy):
        half = SEG // 2
        far, a, b = st.at[dy * 3 + 1], SEG * SLOT[dy, 2], SEG * SLOT[dy, 2] + half
        one = net.go(far.at[0:half], rt.at[dy], at(0, 1))
        two = net.go(far.at[half:SEG], rt.at[4 + dy], at(0, 3))
        relays["t", dy] = (
            (one, rt.at[dy], xb.at[a : a + half], at(0, 1)),
            (two, rt.at[4 + dy], xb.at[b : b + half], at(0, 3)),
        )

    def send_near_t(dy):
        r = SEG * SLOT[dy, 3]
        arrive_t[dy, 3] = [net.go(st.at[dy * 3], xb.at[r : r + SEG], at(0, 1))]
        r = SEG * SLOT[dy, 1]
        arrive_t[dy, 1] = [net.go(st.at[dy * 3 + 2], xb.at[r : r + SEG], at(0, 3))]

    def spread_g(dz):
        src = gout if dz == 0 else gz.at[dz - 1]
        if dz:
            tables_g[dz - 1].wait_recv()
        picks, extra = [], []
        for dy in range(4):
            yy = near(y, dy)
            table = codet[4 * z + yy] if dz == 0 else cgz[dz - 1, yy]
            hot = onehot(table[0:GRP, :])
            weight = jnp.broadcast_to(table[GRP:, None, :], (GRP, CAP, TOK)).reshape(SEG, TOK)
            picks.append(hot)
            extra.append(
                jnp.broadcast_to(jnp.sum(hot * weight, axis=1, keepdims=True), (SEG, 128)).astype(BF)
            )
        pick = jnp.concatenate(picks, axis=0).astype(BF)
        r0 = SEG * SLOT[0, dz]
        gb[r0 : r0 + SEG, D:EXT] = extra[0]
        for dy in (1, 2, 3):
            sg[dz * 3 + dy - 1, :, D:EXT] = extra[dy]

        @pl.loop(0, 4)
        def _(n):
            cols = pl.ds(pl.multiple_of(n * 512, 512), 512)
            rows = jnp.dot(pick, src[:, cols], preferred_element_type=F32).astype(BF)
            gb[r0 : r0 + SEG, cols] = rows[0:SEG]
            for dy in (1, 2, 3):
                sg[dz * 3 + dy - 1, :, cols] = rows[SEG * dy : SEG * (dy + 1)]

    def send_far_g(dz):
        half = SEG // 2
        far, a, b = sg.at[dz * 3 + 1], SEG * SLOT[2, dz], SEG * SLOT[2, dz] + half
        one = net.go(far.at[0:half], rg_relay.at[dz], at(1, 0))
        two = net.go(far.at[half:SEG], rg_relay.at[4 + dz], at(3, 0))
        relays["g", dz] = (
            (one, rg_relay.at[dz], gb.at[a : a + half], at(1, 0)),
            (two, rg_relay.at[4 + dz], gb.at[b : b + half], at(3, 0)),
        )

    def send_near_g(dz):
        r = SEG * SLOT[3, dz]
        arrive_g[3, dz] = [net.go(sg.at[dz * 3], gb.at[r : r + SEG], at(1, 0))]
        r = SEG * SLOT[1, dz]
        arrive_g[1, dz] = [net.go(sg.at[dz * 3 + 2], gb.at[r : r + SEG], at(3, 0))]

    def send_near(step):
        send_near_t(step)
        send_near_g(step)

    def pass_on(step):
        for kind, arrive in (("t", arrive_t), ("g", arrive_g)):
            done = []
            for copy, relay, dst, device in relays[kind, step]:
                copy.wait_recv()
                done.append(net.go(relay, dst, device))
            arrive[(step, 2) if kind == "t" else (2, step)] = done

    def compute(ci):
        rows = pl.ds(ci * CHUNK, CHUNK)
        is_one = member[...] > 0.5
        prob_rows = gb[rows, D : D + 1].astype(F32)

        def ff(n, total):
            start = pl.multiple_of(n * 256, 256)
            cols = pl.ds(start, 256)
            rows_x, gr = xb[rows, :], gb[rows, 0:D]

            def both(a, w):
                zero = jnp.dot(a, w[0], preferred_element_type=F32)
                one = jnp.dot(a, w[1], preferred_element_type=F32)
                return jnp.where(is_one, one, zero)

            down = [wd[8 * e : 8 * e + 8, :, cols].reshape(D, 256) for e in range(2)]
            gate = both(rows_x, [wg[e, :, cols] for e in range(2)])
            up = both(rows_x, [wu[e, :, cols] for e in range(2)])
            back = both(gr, down)
            sig = jax.nn.sigmoid(gate)
            silu = gate * sig
            hidden = (silu * up).astype(BF).astype(F32)
            grad = prob_rows * back
            dgate = grad * up * sig * (1.0 + gate * (1.0 - sig))
            for out, value in ((hb, prob_rows * hidden), (dgb, dgate), (dub, grad * silu)):
                out[rows, cols] = jnp.where(is_one, 0.0, value).astype(BF)
                out[rows, pl.ds(pl.multiple_of(start + F, 256), 256)] = jnp.where(
                    is_one, value, 0.0
                ).astype(BF)
            return total + jnp.sum(hidden * back, axis=1, keepdims=True)

        rp = lax.fori_loop(0, F // 256, ff, jnp.zeros((CHUNK, 1), F32))
        rpb[rows, :] = jnp.broadcast_to(rp, (CHUNK, 128)).astype(BF)

    def row_grads(ci, out):
        rows = pl.ds(ci * CHUNK, CHUNK)

        @pl.loop(0, D // 256)
        def _(n):
            cols = pl.ds(pl.multiple_of(n * 256, 256), 256)
            acc = jnp.zeros((CHUNK, 256), F32)
            for grads, w in ((dgb, wg), (dub, wu)):
                for e in range(2):
                    acc += lax.dot_general(
                        grads[rows, e * F : (e + 1) * F], w[e, cols, :], (((1,), (1,)), ((), ())),
                        preferred_element_type=F32,
                    )
            acc = acc.astype(BF)
            for i, part in enumerate(out):
                size = CHUNK // len(out)
                part[:, cols] = acc[size * i : size * (i + 1)]

    def arrived(ci):
        for place in ORDER[4 * ci : 4 * ci + 4]:
            for arrive in (arrive_t, arrive_g):
                for copy in arrive.get(place, ()):
                    copy.wait_recv()

    returns = []

    def give_back(ci, out):
        per = CHUNK // len(out) // SEG
        for j in range(3, -1, -1):
            i = 4 * ci + j
            dy, dz = ORDER[i]
            q = SEG * SLOT[(4 - dy) % 4, (4 - dz) % 4]
            here_rows = out[j // per].at[SEG * (j % per) : SEG * (j % per + 1)]
            factor = rpb.at[SEG * i : SEG * (i + 1)]
            if i == 0:
                returns.append(copy_local(here_rows, ret_h.at[0:SEG]))
                returns.append(copy_local(factor, retp.at[0:SEG]))
            else:
                pieces.append(net.go(here_rows, ret_h.at[q : q + SEG], columns[i]))
                pieces.append(net.go(factor, retp.at[q : q + SEG], columns[i]))

    pieces = []
    first, second = [ty.at[0], ty.at[1]], [gz.at[0], gz.at[1]]

    def dispatch():
        spread_t(0)
        spread_g(0)
        h = TOK // 2
        t_fwd.wait_recv()
        t_far_a = net.go(ty.at[2, 0:h], ty.at[1, 0:h], at(1, 0))
        g_fwd.wait_recv()
        g_far_a = net.go(gz.at[2, 0:h], gz.at[1, 0:h], at(0, 1))
        t_bwd.wait_recv()
        t_far_b = net.go(ty.at[0, h:TOK], ty.at[1, h:TOK], at(3, 0))
        g_bwd.wait_recv()
        g_far_b = net.go(gz.at[0, h:TOK], gz.at[1, h:TOK], at(0, 3))
        send_far_t(0)
        send_far_g(0)
        send_near(0)
        for step in (3, 1):
            spread_t(step)
            send_far_t(step)
            spread_g(step)
            send_far_g(step)
        for copy in (t_far_a, t_far_b):
            copy.wait_recv()
        spread_t(2)
        send_far_t(2)
        for copy in (g_far_a, g_far_b):
            copy.wait_recv()
        spread_g(2)
        send_far_g(2)
        send_near(3)
        pass_on(0)
        send_near(1)
        pass_on(3)
        send_near(2)
        for copy in weights:
            copy.wait()
        for copy in (t_far_a, t_far_b, g_far_a, g_far_b):
            net.wait_send(copy)
        arrived(0)
        compute(0)
        pass_on(1)
        pass_on(2)
        row_grads(0, first)
        arrived(1)
        compute(1)
        row_grads(1, second)
        arrived(2)
        compute(2)
        arrived(3)
        give_back(0, first)
        give_back(1, second)
        compute(3)
        net.wait_sends(but=pieces)

    dispatch()

    outs = (od, og, ou)
    left, right = (gb, xb, xb), (hb, dgb, dub)
    across, relay_a, relay_b, last_a, last_b = {}, {}, {}, {}, {}
    writes = []

    def reduce():
        def unit(m, dx):
            turn = len(across)
            theirs = wd.at[12 + 2 * (turn % 2) : 14 + 2 * (turn % 2)]

            def part(side):
                owner = near(x, dx) * 2 + side
                cols = pl.ds(pl.multiple_of(owner * 256, 256), 256)
                return lax.dot_general(
                    left[m][:, cols], right[m][...], (((0,), (0,)), ((), ())),
                    preferred_element_type=F32,
                )

            if turn >= 2:
                net.wait_send(list(across.values())[turn - 2])
            value = part(other)
            theirs[0] = value[:, 0:F].astype(BF)
            theirs[1] = value[:, F:].astype(BF)
            across[m, dx] = net.go(theirs, ocr.at[4 * m + dx], (x * 2 + other, c))
            value = part(core)
            across[m, dx].wait_recv()
            both = ocr.at[4 * m + dx]
            both[0] = (value[:, 0:F] + both[0].astype(F32)).astype(BF)
            both[1] = (value[:, F:] + both[1].astype(F32)).astype(BF)
            if dx == 2:
                relay_a[m] = net.go(both.at[0], rlr.at[2 * m], along(1))
                relay_b[m] = net.go(both.at[1], rlr.at[2 * m + 1], along(3))

        def fold(m):
            relay_a[m].wait_recv()
            relay_b[m].wait_recv()
            a, b = ocr.at[4 * m + 1], ocr.at[4 * m + 3]
            a[0] = (a[0].astype(F32) + rlr[2 * m].astype(F32)).astype(BF)
            last_a[m] = net.go(a, wd.at[4 * m : 4 * m + 2], along(1))
            b[1] = (b[1].astype(F32) + rlr[2 * m + 1].astype(F32)).astype(BF)
            last_b[m] = net.go(b, wd.at[4 * m + 2 : 4 * m + 4], along(3))

        def finish(m):
            last_a[m].wait_recv()
            last_b[m].wait_recv()
            mine = ocr.at[4 * m]
            mine[...] = (
                mine[...].astype(F32)
                + wd[4 * m : 4 * m + 2].astype(F32)
                + wd[4 * m + 2 : 4 * m + 4].astype(F32)
            ).astype(BF)
            writes.append(copy_local(mine, outs[m]))

        third, fourth = [st.at[i] for i in range(4)], [st.at[4 + i] for i in range(4)]
        for do in PLAN:
            if do[0] == "p":
                fold(int(do[1]))
            elif do == "r2":
                row_grads(2, third)
                give_back(2, third)
            elif do == "r3":
                row_grads(3, fourth)
                give_back(3, fourth)
            else:
                unit(int(do[0]), int(do[1]))

        for copy in returns:
            copy.wait()
        for copy in pieces:
            copy.wait_recv()
        back = copy_local(ret_h, gb.at[:, 0:D])
        for copy in pieces:
            net.wait_send(copy)
        pall = rpb
        lane = lax.broadcasted_iota(jnp.int32, (SEG, 128), 1)
        group = lax.broadcasted_iota(jnp.int32, (SEG, 128), 0) // CAP
        spread = []
        for s, (dy, dz) in enumerate(ORDER):
            col = near(y, dy) * 4 + near(z, dz)
            pall[s * SEG : (s + 1) * SEG, :] = onehot(code[col, 0:GRP, :]).astype(BF)
            value = retp[s * SEG : (s + 1) * SEG, :].astype(F32)
            spread.append(jnp.where(lane == group + col * GRP, value, 0.0))
        over_rows = (((0,), (0,)), ((), ()))
        per_dest = lax.dot_general(
            jnp.concatenate(spread, axis=0).astype(BF), pall[...], over_rows,
            preferred_element_type=F32,
        )
        number = lax.broadcasted_iota(jnp.int32, (GRP * COL, TOK), 0).astype(F32)
        for k in range(TOPK):
            mine = jnp.where(number == destk[k : k + 1, :], per_dest, 0.0)
            gp_o[k : k + 1, :] = jnp.sum(mine, axis=0, keepdims=True).astype(BF)
        back.wait()
        total = lax.dot_general(
            pall[...], gb[:, 0:D], over_rows, preferred_element_type=F32
        ).astype(BF)
        for i in range(4):
            rt[i] = total[32 * i : 32 * (i + 1)]
            writes.append(copy_local(rt.at[i], gt_o.at[32 * i : 32 * (i + 1)]))
        for m in range(3):
            finish(m)
        net.wait_sends()
        for copy in writes:
            copy.wait()

    reduce()


PLAN = [
    "02", "12", "22", "01", "03", "p0", "r2", "11", "13", "p1", "r3", "21", "23", "p2", "00", "10", "20",
]


def widen_kernel(a, b, c, rows, probs, wide_a, wide_b, wide_c, rows_o, probs_o):
    for narrow, wide in ((a, wide_a), (b, wide_b), (c, wide_c)):
        wide[...] = narrow[...].astype(F32)
    rows_o[...] = rows[...]
    probs_o[...] = probs[...]


def body(tokens, grad_out, probs, expert_ids, serve_map, replica_pick, w_gate, w_up, w_down):
    wide = lambda n, w, dt=BF: jax.ShapeDtypeStruct((n, w), dt)
    vmem = lambda *s, dt=BF: pltpu.VMEM(s, dt)
    dma = lambda n: pltpu.SemaphoreType.DMA((n,))
    out = jax.ShapeDtypeStruct((2, 256, F), BF)
    gp, gt, og, ou, od, _ = pl.pallas_call(
        layer_kernel,
        out_shape=[wide(TOPK, TOK), wide(TOK, D), out, out, out, wide(ROWS, D)],
        in_specs=[VM] * 6 + [ANY] * 3,
        out_specs=[VM] + [ANY] * 5,
        scratch_shapes=[
            vmem(2, D, F), vmem(2, D, F), vmem(16, 256, F), vmem(ROWS, D), vmem(ROWS, EXT),
            vmem(3, TOK, D), vmem(3, TOK, D),
            vmem(COL, 16, TOK, dt=F32), vmem(COL, 16, TOK, dt=F32),
            vmem(3, 4, 16, TOK, dt=F32), vmem(3, 4, 16, TOK, dt=F32),
            vmem(12, SEG, D), vmem(12, SEG, EXT), vmem(8, SEG // 2, D), vmem(8, SEG // 2, EXT),
            vmem(ROWS, 2 * F), vmem(ROWS, 2 * F), vmem(ROWS, 2 * F), vmem(ROWS, 128), vmem(ROWS, 128),
            vmem(CHUNK, 1, dt=F32), vmem(8, TOK, dt=F32),
            vmem(12, 2, 256, F), vmem(6, 256, F),
            dma(NCOPY), dma(NCOPY), dma(40),
        ],
        compiler_params=pltpu.CompilerParams(
            collective_id=0, has_side_effects=True, vmem_limit_bytes=64 * 2**20
        ),
        name="layer",
    )(tokens, grad_out, expert_ids.T, replica_pick.T, probs.T, serve_map, w_gate, w_up, w_down)
    blocks = [pl.BlockSpec((1, 128, F), lambda i: (i // 2, i % 2, 0))] * 3
    blocks += [pl.BlockSpec((TOK // 4, D), lambda i: (i, 0)), pl.BlockSpec((TOPK, TOK), lambda i: (0, 0))]
    wide_out = jax.ShapeDtypeStruct((2, 256, F), F32)
    og, ou, od, gt, gp = pl.pallas_call(
        widen_kernel,
        grid=(4,),
        out_shape=[wide_out] * 3 + [wide(TOK, D), wide(TOPK, TOK)],
        in_specs=blocks,
        out_specs=blocks,
        name="widen",
    )(og, ou, od, gt, gp)
    return (gt, gp.T, og, ou, od)


def solution(mesh):
    rows = P(("grp", "exp"), None)
    by_expert = P("exp", None, None)
    return jax.shard_map(
        body,
        mesh=mesh,
        in_specs=(rows, rows, rows, rows, P(), rows, by_expert, by_expert, by_expert),
        out_specs=(rows, rows) + (P("exp", "grp", None),) * 3,
        check_vma=False,
    )
```
